32 devices in a mesh: slab: 2 (over y), col: 4 (over x, core), row: 4 (over z).
Axes of the slice: x: 2, y: 2, z: 4, core: 2. Of those that a mesh axis runs over, the one named last changes fastest.
Arguments:
- tokens: bfloat16 [256, 256, 384], P(('slab', 'row'), 'col'), parts along dimension 0, may hold values from -6 to 6
- norm_gain: float32 [384], replicated, may hold values from 0.1 to 1.9
- query_weight: bfloat16 [384, 384], replicated, may hold values from -0.3125 to 0.3125
- key_weight: bfloat16 [384, 384], replicated, may hold values from -0.3125 to 0.3125
- value_weight: bfloat16 [384, 384], replicated, may hold values from -0.3125 to 0.3125
- out_weight: bfloat16 [384, 384], replicated, may hold values from -0.3125 to 0.3125
- head_scale: float32 [6], replicated, may hold values from 4 to 12
- counts: int32 [32, 16], P(('slab', 'row'), 'col'), parts along dimension 0, may hold values from 0 to 4, as said below
- sources: int32 [32, 16, 4], P(('slab', 'row'), 'col'), parts along dimension 0, may hold values from 0 to 255, as said below
Outputs:
- inpainted: bfloat16 [256, 256, 384], P(('slab', 'row'), 'col'), parts along dimension 0
The draws below stay inside these ranges and needn't reach their ends.
There are 2 independent parts, one for each index of `slab`. The reference program is written for one: setup_inputs(seed, part) draws one part's arguments, and reference() takes and returns one part's arrays. A program takes and returns all parts, laid end to end along the dimension named above; an argument that names none is the same for every part. Nothing has to cross between parts.
Inputs may be any that keep to these rules, and one draw needn't show every extreme that they name: `counts`: each block of 4 x 4 tiles whose first tile row and column are multiples of 4 and 4 has at least the smaller of 4 and 8 and at most 8 tiles with a count above 0. `sources`: every entry names a tile of the same band of 4 tile rows as its own tile (the same tile row divided by 4). Entry j of tile t with j below counts[t] names a tile whose count is 0; the other entries are arbitrary tiles of that band. Among the entries below the counts of all tiles of one block of 4 x 4 tiles, at most 8 name tiles of any one block of 4 tile columns.
All inputs are finite; a program needn't handle non-finite values.
Results may differ from the reference program's by a relative error of at most 0.0041.
Values may be sent and summed in bfloat16 or wider, within the bound.
No kernel may reach another device: no remote copies, remote signals or barrier semaphores. Data moves between devices by JAX's collectives and lax.ppermute only.
A program may use at most 192 MiB of HBM per device.

```python
import math
import jax
import jax.numpy as jnp
from jax import lax

D = 384
HEADS = 6
TILE_ROWS = 8
TILE_COLS = 16
RADIUS = 3
S_MAX = 4
MASK_MOST = 8
NR = 128
NC = 256
TR = 16
TC = 16
TR_DEV = 4
TC_DEV = 4
CAP = 8


def tile_plan(base_key):
    band_count = TR // TR_DEV
    col_count = TC // TC_DEV
    per_device = TR_DEV * TC_DEV
    capacity = CAP
    subkeys = jax.random.split(jax.random.fold_in(base_key, 7), 8)
    masked_many = jax.random.randint(subkeys[0], (band_count, col_count), min(4, MASK_MOST), MASK_MOST + 1)
    forced = jax.random.randint(subkeys[1], (band_count,), 0, col_count)
    is_forced = jnp.arange(col_count)[None, :] == forced[:, None]
    masked_many = jnp.where(is_forced, MASK_MOST, masked_many)
    tile_scores = jax.random.randint(subkeys[2], (band_count, col_count, per_device), 0, 1 << 20) * per_device + jnp.arange(per_device)
    tile_order = jnp.argsort(tile_scores, axis=-1)
    tile_rank = jnp.argsort(tile_order, axis=-1)
    masked = tile_rank < masked_many[:, :, None]
    counts = jax.random.randint(subkeys[3], (band_count, col_count, per_device), min(2, S_MAX), S_MAX + 1)
    counts = jnp.where(is_forced[:, :, None] & (tile_rank == 0), S_MAX, counts)
    counts = jnp.where(masked, counts, 0)
    entry_start = jnp.cumsum(counts, axis=-1) - counts
    entry_index = entry_start[..., None] + jnp.arange(S_MAX)
    live_mask = jnp.arange(S_MAX) < counts[..., None]
    slot_total = col_count * capacity
    receiver = jax.random.randint(subkeys[4], (band_count,), 0, col_count)
    slot_ids = jnp.arange(slot_total)
    slot_scores = jax.random.randint(subkeys[5], (band_count, col_count, slot_total), 0, 1 << 20) * slot_total + slot_ids
    first_slots = (slot_ids // capacity)[None, None, :] == receiver[:, None, None]
    slot_scores = jnp.where(first_slots, slot_ids % capacity - capacity, slot_scores)
    slot_order = jnp.argsort(slot_scores, axis=-1)
    entry_clip = jnp.minimum(entry_index, slot_total - 1).reshape(band_count, col_count, -1)
    owner_col = (jnp.take_along_axis(slot_order, entry_clip, axis=-1) // capacity).reshape(entry_index.shape)
    band_rows = jnp.arange(band_count)[:, None, None, None]
    owner_many = masked_many[band_rows, owner_col]
    pick_free = jax.random.randint(subkeys[6], entry_index.shape, 0, per_device - owner_many)
    cum_free = jnp.cumsum(1 - masked.astype(jnp.int32), axis=-1)
    owner_cum = cum_free[band_rows, owner_col]
    local_tile = jnp.sum((owner_cum <= pick_free[..., None]).astype(jnp.int32), axis=-1)
    tile_row = band_rows * TR_DEV + local_tile // TC_DEV
    tile_col = owner_col * TC_DEV + local_tile % TC_DEV
    live_ids = tile_row * TC + tile_col
    dead_ids = band_rows * TR_DEV * TC + jax.random.randint(subkeys[7], entry_index.shape, 0, TR_DEV * TC)
    sources = jnp.where(live_mask, live_ids, dead_ids)
    counts = counts.reshape(band_count, col_count, TR_DEV, TC_DEV).transpose(0, 2, 1, 3).reshape(TR, TC)
    sources = sources.reshape(band_count, col_count, TR_DEV, TC_DEV, S_MAX).transpose(0, 2, 1, 3, 4).reshape(TR, TC, S_MAX)
    return (counts.astype(jnp.int32), sources.astype(jnp.int32))


def draw_counts(key, part):
    return tile_plan(key)[0]


def draw_sources(key, part):
    return tile_plan(key)[1]


def block_scale(rng, shape, cuts, smallest, top_value):
    level = 1.0
    for dim, parts in cuts:
        steps = jax.random.uniform(jax.random.fold_in(jax.random.fold_in(rng, 6), dim), (parts,), jnp.float32, smallest / len(cuts), top_value / len(cuts))
        level = level * jnp.repeat(jnp.exp(steps), shape[dim] // parts).reshape((-1,) + (1,) * (len(shape) - 1 - dim))
    return level


def noise(key, extent, scale, limit, pieces=(), kind=jnp.bfloat16):
    array = scale * jax.random.normal(key, extent, jnp.float32)
    if pieces:
        array = array * block_scale(key, extent, pieces, -0.22, 0.18)
    return jnp.clip(array, -limit, limit).astype(kind)


def setup_inputs(seed: int = 0, part: int = 0) -> dict:
    splits = jax.random.split(jax.random.key(seed), 10)
    own_keys = jax.random.split(jax.random.fold_in(splits[9], part), 10)
    return {
        "tokens": noise(own_keys[0], (NR, NC, D), 1.0, 6.0, ((0, 4), (1, 4))),
        "norm_gain": jnp.clip(1.0 + 0.18 * jax.random.normal(splits[1], (D,), jnp.float32), 0.1, 1.9),
        "query_weight": noise(splits[2], (D, D), D ** -0.5, 0.3125),
        "key_weight": noise(splits[3], (D, D), D ** -0.5, 0.3125),
        "value_weight": noise(splits[4], (D, D), D ** -0.5, 0.3125),
        "out_weight": noise(splits[5], (D, D), D ** -0.5, 0.3125),
        "head_scale": jnp.clip(jnp.exp(jax.random.uniform(splits[6], (HEADS,), jnp.float32, math.log(4.0), math.log(12.0))), 4.0, 12.0),
        "counts": draw_counts(jax.random.fold_in(jax.random.fold_in(splits[9], part), 71), part),
        "sources": draw_sources(jax.random.fold_in(jax.random.fold_in(splits[9], part), 71), part),
    }


def normalize(flat_tokens, norm_gain):
    as_float = flat_tokens.astype(jnp.float32)
    inverse_rms = lax.rsqrt(lax.optimization_barrier(jnp.mean(as_float * as_float, axis=-1, keepdims=True)) + 1e-06)
    return (as_float * inverse_rms * norm_gain).astype(jnp.bfloat16)

def unit_heads(projected, head_factor):
    split_heads = projected.reshape(projected.shape[0], head_factor.shape[0], -1)
    inverse_len = lax.rsqrt(lax.optimization_barrier(jnp.sum(split_heads * split_heads, axis=-1, keepdims=True)) + 1e-06)
    return (split_heads * inverse_len * head_factor[:, None]).reshape(projected.shape).astype(jnp.bfloat16)

def to_tiles(grid_flat, tile_rows, tile_cols):
    feature = grid_flat.shape[-1]
    shaped = grid_flat.reshape(tile_rows, TILE_ROWS, tile_cols, TILE_COLS, feature)
    return shaped.transpose(0, 2, 1, 3, 4).reshape(tile_rows * tile_cols, TILE_ROWS * TILE_COLS, feature)

def near_band():
    win_rows = TILE_ROWS + 2 * RADIUS
    win_cols = TILE_COLS + 2 * RADIUS
    query_pos = jnp.arange(TILE_ROWS * TILE_COLS, dtype=jnp.int32)
    key_pos = jnp.arange(win_rows * win_cols, dtype=jnp.int32)
    query_row = (query_pos // TILE_COLS)[:, None]
    query_col = (query_pos % TILE_COLS)[:, None]
    key_row = (key_pos // win_cols)[None, :]
    key_col = (key_pos % win_cols)[None, :]
    inside = (key_row >= query_row) & (key_row <= query_row + 2 * RADIUS) & (key_col >= query_col) & (key_col <= query_col + 2 * RADIUS)
    return inside.astype(jnp.float32)

def windows(padded, row_index):
    win_rows = TILE_ROWS + 2 * RADIUS
    win_cols = TILE_COLS + 2 * RADIUS
    row_strip = lax.dynamic_slice_in_dim(padded, row_index * TILE_ROWS, win_rows, 0)
    blocks = row_strip.shape[1] // TILE_COLS - 1
    split_cols = row_strip.reshape(win_rows, blocks + 1, TILE_COLS, row_strip.shape[-1])
    joined = jnp.concatenate([split_cols[:, :blocks], split_cols[:, 1:, :2 * RADIUS]], axis=2)
    return joined.transpose(1, 0, 2, 3).reshape(blocks, win_rows * win_cols, row_strip.shape[-1])

def attend(query_tile, key_tile, value_tile, allowed):
    query_heads = query_tile.reshape(query_tile.shape[0], query_tile.shape[1], HEADS, -1).astype(jnp.float32)
    key_heads = key_tile.reshape(key_tile.shape[0], key_tile.shape[1], HEADS, -1).astype(jnp.float32)
    value_heads = value_tile.reshape(value_tile.shape[0], value_tile.shape[1], HEADS, -1).astype(jnp.float32)
    scores = jnp.einsum('tqhd,tkhd->thqk', query_heads, key_heads)
    weights = jnp.exp(scores) * allowed[:, None]
    weight_total = lax.optimization_barrier(jnp.sum(weights, axis=-1)).transpose(0, 2, 1)
    rounded = lax.optimization_barrier(weights.astype(jnp.bfloat16))
    summed = jnp.einsum('thqk,tkhd->tqhd', rounded.astype(jnp.float32), value_heads)
    return (summed, weight_total)

def reference(tokens, norm_gain, query_weight, key_weight, value_weight, out_weight, head_scale, counts, sources):
    tile_size = TILE_ROWS * TILE_COLS
    flat_tokens = tokens.reshape(NR * NC, D)
    normed = normalize(flat_tokens, norm_gain)
    unit_scale = jnp.ones((HEADS,), jnp.float32)
    key_rows = unit_heads(jnp.dot(normed, key_weight, preferred_element_type=jnp.float32), unit_scale)
    value_rows = jnp.dot(normed, value_weight, preferred_element_type=jnp.float32).astype(jnp.bfloat16)
    valid_cells = jnp.repeat(jnp.repeat((counts == 0).astype(jnp.float32), TILE_ROWS, axis=0), TILE_COLS, axis=1)
    pad_widths = ((RADIUS, RADIUS), (RADIUS, TILE_COLS - RADIUS), (0, 0))
    near_keys = jnp.pad(key_rows.reshape(NR, NC, D), pad_widths)
    near_values = jnp.pad(value_rows.reshape(NR, NC, D), pad_widths)
    near_valid = jnp.pad(valid_cells[..., None], pad_widths)
    key_tiles = to_tiles(key_rows, TR, TC)
    value_tiles = to_tiles(value_rows, TR, TC)
    band_mask = near_band()
    normed_grid = normed.reshape(NR, NC, D)

    def one_row(row_index):
        row_normed = lax.dynamic_slice_in_dim(normed_grid, row_index * TILE_ROWS, TILE_ROWS, 0).reshape(-1, D)
        query_rows = unit_heads(jnp.dot(row_normed, query_weight, preferred_element_type=jnp.float32), head_scale)
        query_tile = to_tiles(query_rows, 1, TC)
        valid_win = windows(near_valid, row_index)[..., 0]
        near_sum, near_total = attend(query_tile, windows(near_keys, row_index), windows(near_values, row_index), band_mask[None] * valid_win[:, None, :])
        row_sources = lax.dynamic_index_in_dim(sources, row_index, 0, keepdims=False)
        row_counts = lax.dynamic_index_in_dim(counts, row_index, 0, keepdims=False)
        far_keys = jnp.take(key_tiles, row_sources.reshape(-1), axis=0).reshape(TC, S_MAX * tile_size, D)
        far_values = jnp.take(value_tiles, row_sources.reshape(-1), axis=0).reshape(TC, S_MAX * tile_size, D)
        live_weight = (jnp.arange(S_MAX, dtype=jnp.int32)[None, :] < row_counts[:, None]).astype(jnp.float32)
        allowed = jnp.repeat(live_weight, tile_size, axis=1)[:, None, :]
        far_sum, far_total = attend(query_tile, far_keys, far_values, allowed)
        attended = ((near_sum + far_sum) / (near_total + far_total)[..., None]).astype(jnp.bfloat16)
        attended = attended.reshape(TC, TILE_ROWS, TILE_COLS, D).transpose(1, 0, 2, 3).reshape(-1, D)
        row_tokens = lax.dynamic_slice_in_dim(tokens, row_index * TILE_ROWS, TILE_ROWS, 0).reshape(-1, D)
        mixed_rows = row_tokens.astype(jnp.float32) + jnp.dot(attended, out_weight, preferred_element_type=jnp.float32)
        return mixed_rows.astype(jnp.bfloat16).reshape(TILE_ROWS, NC, D)
    inpainted = lax.map(one_row, jnp.arange(TR, dtype=jnp.int32))
    return inpainted.reshape(NR, NC, D)
```

```python
import functools
import math
import jax
import jax.numpy as jnp
from jax import lax
from jax.experimental import pallas as pl
from jax.experimental.pallas import tpu as pltpu
from jax.sharding import PartitionSpec as P

HEADS = 6
TILE_ROWS = 8
TILE_COLS = 16
RADIUS = 3
S_MAX = 4
MASK_MOST = 8
SIDE = 8
MARK = 1024.0
MARK_LEVEL = 1000.0
LATE_TILES = 4
LOG2E = math.log2(math.e)
F32 = jnp.float32
BF16 = jnp.bfloat16


def pair_swap(low, high, axis):
    count = lax.axis_size(axis)
    index = lax.axis_index(axis)
    even = index % 2 == 0
    first = [(i, i + 1) for i in range(0, count - 1, 2)]
    second = [(i, i + 1) for i in range(1, count - 1, 2)]
    both = lambda pairs: pairs + [(b, a) for a, b in pairs]
    one = lax.ppermute(jnp.where(even, high, low), axis, both(first))
    two = lax.ppermute(jnp.where(even, low, high), axis, both(second))
    mark = jnp.asarray(MARK, low.dtype)
    before = jnp.where(index == 0, mark, jnp.where(even, two, one))
    after = jnp.where(index == count - 1, mark, jnp.where(even, one, two))
    return before, after


def spread(array, axis):
    count = lax.axis_size(axis)
    held = {0: array}
    bit = count // 2
    while bit:
        pairs = [(i, i ^ bit) for i in range(count)]
        held.update({rel ^ bit: lax.ppermute(item, axis, pairs) for rel, item in held.items()})
        bit //= 2
    return held


def pack_kernel(tile_cols, keep, counts_ref, tokens_ref, *chunk_refs):
    tile_rows = tokens_ref.shape[0] // TILE_ROWS
    free = jnp.int32(0)
    for t in range(tile_rows * tile_cols):
        free = free + (counts_ref[t // tile_cols, t % tile_cols] == 0).astype(jnp.int32)
    seen_free = jnp.int32(0)
    seen_masked = jnp.int32(0)
    for t in range(tile_rows * tile_cols):
        a, b = t // tile_cols, t % tile_cols
        is_free = (counts_ref[a, b] == 0).astype(jnp.int32)
        rank = jnp.where(is_free == 1, seen_free, free + seen_masked)
        seen_free = seen_free + is_free
        seen_masked = seen_masked + 1 - is_free
        low = 0
        for ref in chunk_refs:
            size = ref.shape[0]

            @pl.when((rank >= low) & (rank < low + size))
            def _(ref=ref, low=low, a=a, b=b, rank=rank):
                ref[rank - low] = tokens_ref[
                    TILE_ROWS * a : TILE_ROWS * (a + 1), TILE_COLS * b : TILE_COLS * (b + 1), :
                ].reshape(TILE_ROWS * TILE_COLS, tokens_ref.shape[-1])

            low += size


def head_blocks(feature):
    size = feature // HEADS
    row = lax.broadcasted_iota(jnp.int32, (feature, feature), 0) // size
    col = lax.broadcasted_iota(jnp.int32, (feature, feature), 1) // size
    return jnp.where(row == col, 1.0, 0.0).astype(BF16)


def unit(projected, blocks):
    squares = (projected * projected).astype(BF16)
    total = jnp.dot(squares, blocks, preferred_element_type=F32)
    return projected * lax.rsqrt(total + 1e-6)


def normed_of(raw, gain):
    level = jnp.mean(raw * raw, axis=-1, keepdims=True)
    return raw * lax.rsqrt(level + 1e-6) * gain, level


def contract_last(left, right):
    return lax.dot_general(left, right, (((1,), (1,)), ((), ())), preferred_element_type=F32)


def near_kernel(
    counts_ref, tokens_ref, tail_ref, top_ref, bottom_ref, gain_ref, scale_ref,
    wq_ref, wk_ref, wv_ref, wo_ref,
    out_ref, acc_ref, mq_ref,
    keys, values, valid, queries, blocks,
):
    grid_rows, grid_cols, feature = tokens_ref.shape
    tile_rows = grid_rows // TILE_ROWS
    tile_cols = grid_cols // TILE_COLS
    wide = tail_ref.shape[1] + grid_cols
    lanes = 2 * feature // HEADS
    win_rows = TILE_ROWS + 2 * RADIUS
    blocks[...] = head_blocks(feature)

    def put_keys(raw, own_valid, places):
        rows = raw.shape[0]
        normed, level = normed_of(raw, gain_ref[...][None])
        ok = jnp.where(level < MARK_LEVEL, own_valid, 0.0)
        ok = pltpu.roll(jnp.broadcast_to(ok, (rows, wide, lanes)), RADIUS, 1)
        shifted = pltpu.roll(normed, RADIUS, 1).astype(BF16).reshape(rows * wide, feature)
        key = unit(jnp.dot(shifted, wk_ref[...], preferred_element_type=F32), blocks[...])
        value = jnp.dot(shifted, wv_ref[...], preferred_element_type=F32)
        value = value * jnp.concatenate([ok] * (feature // lanes), axis=-1).reshape(value.shape)
        key = key.reshape(rows, wide, feature)
        value = value.reshape(rows, wide, feature)
        for side in range(2):
            low = side * SIDE
            for at, start, size in places:
                into = (side, pl.ds(at, size))
                keys[into] = key[start : start + size, low : low + grid_cols].astype(BF16)
                values[into] = value[start : start + size, low : low + grid_cols].astype(BF16)
                valid[into] = ok[start : start + size, low : low + grid_cols].astype(BF16)
        return normed

    edge = jnp.concatenate([top_ref[...], bottom_ref[...]], axis=0).astype(F32)
    put_keys(edge, 1.0, ((0, 0, RADIUS), (RADIUS + grid_rows, RADIUS, RADIUS)))

    def project(a, carry):
        rows = pl.ds(a * TILE_ROWS, TILE_ROWS)
        raw = jnp.concatenate([tokens_ref[rows], tail_ref[rows]], axis=1).astype(F32)
        tile = lax.broadcasted_iota(jnp.int32, (1, wide, 1), 1) // TILE_COLS
        own_valid = jnp.ones((1, wide, 1), F32)
        for b in range(tile_cols):
            flag = jnp.where(counts_ref[a, b] == 0, 1.0, 0.0)
            own_valid = jnp.where(tile == b, flag, own_valid)
        normed = put_keys(raw, own_valid, ((RADIUS + a * TILE_ROWS, 0, TILE_ROWS),))
        flat = normed[:, :grid_cols].astype(BF16).reshape(TILE_ROWS * grid_cols, feature)
        query = unit(jnp.dot(flat, wq_ref[...], preferred_element_type=F32), blocks[...])
        query = (query * scale_ref[...]).reshape(TILE_ROWS, grid_cols // SIDE, SIDE, feature)
        for c in range(grid_cols // SIDE):
            queries[a, c] = query[:, c].reshape(TILE_ROWS * SIDE, feature).astype(BF16)
        return carry

    lax.fori_loop(0, tile_rows, project, 0)

    tokens_of_side = TILE_ROWS * SIDE
    window = win_rows * TILE_COLS
    qpos = lax.broadcasted_iota(jnp.int32, (2 * tokens_of_side, window), 0) % tokens_of_side
    kpos = lax.broadcasted_iota(jnp.int32, (2 * tokens_of_side, window), 1)
    down = kpos // TILE_COLS - qpos // SIDE
    across = kpos % TILE_COLS - qpos % SIDE
    inside = (down >= 0) & (down <= 2 * RADIUS) & (across >= 0) & (across <= 2 * RADIUS)
    band = jnp.where(inside, 1.0, 0.0).astype(BF16)
    first = lax.broadcasted_iota(jnp.int32, (tokens_of_side, lanes), 1) < lanes // 2
    zero = jnp.zeros((tokens_of_side, lanes), BF16)

    def attend(t, slot):
        a = t // tile_cols
        b = t % tile_cols
        nums, dens = [], []
        for side in range(2):
            query = queries[a, 2 * b + side]
            at = (side, pl.ds(a * TILE_ROWS, win_rows), pl.ds(pl.multiple_of(b * TILE_COLS, TILE_COLS), TILE_COLS))
            ok = valid[at].reshape(window, lanes)
            num, den = [], []
            for p in range(feature // lanes):
                part = slice(p * lanes, (p + 1) * lanes)
                key = keys[(*at, part)].reshape(window, lanes)
                value = jnp.concatenate([values[(*at, part)].reshape(window, lanes), ok], axis=1)
                q = query[:, part]
                stacked = jnp.concatenate([jnp.where(first, q, zero), jnp.where(first, zero, q)], axis=0)
                weights = jnp.exp2(contract_last(stacked, key)).astype(BF16) * band
                both = jnp.dot(weights, value, preferred_element_type=F32)
                num.append(jnp.where(first, both[:tokens_of_side, :lanes], both[tokens_of_side:, :lanes]))
                den.append(jnp.where(first, both[:tokens_of_side, lanes:], both[tokens_of_side:, lanes:]))
            nums.append(jnp.concatenate(num, axis=1))
            dens.append(jnp.concatenate(den, axis=1))
        masked = counts_ref[a, b] > 0

        @pl.when(masked)
        def _():
            for side in range(2):
                part = slice(side * tokens_of_side, (side + 1) * tokens_of_side)
                acc_ref[slot, 0, part] = nums[side]
                acc_ref[slot, 1, part] = dens[side]
                mq_ref[slot, part] = queries[a, 2 * b + side]

        @pl.when(jnp.logical_not(masked))
        def _():
            finish(a, b, nums, dens, tokens_ref, wo_ref, out_ref.at[
                pl.ds(a * TILE_ROWS, TILE_ROWS), pl.ds(pl.multiple_of(b * TILE_COLS, TILE_COLS), TILE_COLS)])

        return slot + masked.astype(jnp.int32)

    lax.fori_loop(0, tile_rows * tile_cols, attend, jnp.int32(0))


def finish(a, b, nums, dens, tokens_ref, wo_ref, into):
    feature = tokens_ref.shape[-1]
    sides = [(n / d).reshape(TILE_ROWS, SIDE, feature) for n, d in zip(nums, dens)]
    attended = jnp.concatenate(sides, axis=1).reshape(TILE_ROWS * TILE_COLS, feature).astype(BF16)
    raw = tokens_ref[
        pl.ds(a * TILE_ROWS, TILE_ROWS), pl.ds(pl.multiple_of(b * TILE_COLS, TILE_COLS), TILE_COLS)
    ].reshape(TILE_ROWS * TILE_COLS, feature).astype(F32)
    mixed = raw + jnp.dot(attended, wo_ref[...], preferred_element_type=F32)
    into[...] = mixed.astype(BF16).reshape(TILE_ROWS, TILE_COLS, feature)


def far_kernel(plan, last, all_cols, axes, *refs):
    col_count = len(plan["rels"])
    me_ref, counts_ref, sources_ref = refs[:3]
    refs = refs[3:]
    rel_counts = dict(zip(plan["rels"], refs[:col_count]))
    refs = refs[col_count:]
    chunks = list(zip(plan["chunks"], refs[: len(plan["chunks"])]))
    refs = refs[len(plan["chunks"]) :]
    mq_ref, acc_in_ref, gain_ref, wk_ref, wv_ref = refs[:5]
    refs = refs[5:]
    if last:
        tokens_ref, wo_ref, _, out_ref = refs[:4]
        refs = refs[4:]
    else:
        acc_out_ref = refs[0]
        refs = refs[1:]
    keys, values, blocks, raw, acc_ref, needed, place, todo, todo_count, tile_of = refs[:10]
    refs = refs[10:]
    if last:
        staged, sems = refs
    tile_rows, tile_cols = counts_ref.shape
    tiles = tile_rows * tile_cols
    tile_size, feature = raw.shape[1:]
    lanes = 2 * feature // HEADS
    blocks[...] = head_blocks(feature)
    my_col = me_ref[0]
    my_band = me_ref[1]

    def clear(i, carry):
        place[i] = -1
        return carry

    lax.fori_loop(0, col_count * tiles, clear, 0)

    def plan_tile(t, carry):
        count, slot = carry
        a, b = t // tile_cols, t % tile_cols
        live = counts_ref[a, b]

        @pl.when(live > 0)
        def _():
            tile_of[slot] = t
            todo_count[slot] = 0

        def plan_entry(j, count):
            source = sources_ref[a, b, j]
            col = source % all_cols
            rel = (col // tile_cols) ^ my_col
            sa = source // all_cols - my_band * tile_rows
            sb = col % tile_cols
            local = sa * tile_cols + sb

            def rank_in(ref):
                def step(i, rank):
                    return rank + (ref[i // tile_cols, i % tile_cols] == 0).astype(jnp.int32)

                return lax.fori_loop(0, local, step, jnp.int32(0))

            rank = jnp.int32(0)
            for known, ref in rel_counts.items():
                rank = lax.cond(rel == known, functools.partial(rank_in, ref), lambda rank=rank: rank)
            here = jnp.bool_(False)
            for (known, low, size), _ in chunks:
                here = here | ((rel == known) & (rank >= low) & (rank < low + size))
            name = rel * tiles + rank
            fresh = here & (place[name] < 0)

            @pl.when(fresh)
            def _():
                place[name] = count
                needed[count] = name

            @pl.when(here)
            def _():
                n = todo_count[slot]
                todo[slot, n] = place[name]
                todo_count[slot] = n + 1

            return count + fresh.astype(jnp.int32)

        count = lax.fori_loop(0, live, plan_entry, count)
        return count, slot + (live > 0).astype(jnp.int32)

    count, slots = lax.fori_loop(0, tiles, plan_tile, (jnp.int32(0), jnp.int32(0)))

    def fetch(i, k):
        name = needed[i]
        rel, rank = name // tiles, name % tiles
        for (known, low, size), ref in chunks:
            @pl.when((rel == known) & (rank >= low) & (rank < low + size))
            def _(ref=ref, low=low):
                raw[k] = ref[rank - low]

    def project(i, carry):
        fetch(2 * i, 0)
        fetch(jnp.minimum(2 * i + 1, count - 1), 1)
        flat = raw[...].reshape(2 * tile_size, feature).astype(F32)
        normed = normed_of(flat, gain_ref[...])[0].astype(BF16)
        key = unit(jnp.dot(normed, wk_ref[...], preferred_element_type=F32), blocks[...]).astype(BF16)
        value = jnp.dot(normed, wv_ref[...], preferred_element_type=F32).astype(BF16)
        keys[pl.ds(2 * i, 2)] = key.reshape(2, tile_size, feature)
        values[pl.ds(2 * i, 2)] = value.reshape(2, tile_size, feature)
        return carry

    lax.fori_loop(0, (count + 1) // 2, project, 0)

    first = lax.broadcasted_iota(jnp.int32, (tile_size, lanes), 1) < lanes // 2
    zero = jnp.zeros((tile_size, lanes), BF16)

    def attend(slot, carry):
        have = todo_count[slot]
        acc_ref[...] = acc_in_ref[slot]

        def step(i, carry):
            two = 2 * i + 1 < have
            one = todo[slot, 2 * i]
            other = todo[slot, jnp.where(two, 2 * i + 1, 2 * i)]
            there = jnp.where(two, 1.0, 0.0).astype(BF16)
            query = mq_ref[slot]
            ones = jnp.ones((tile_size, lanes), BF16)
            for p in range(feature // lanes):
                part = slice(p * lanes, (p + 1) * lanes)
                key = jnp.concatenate([keys[one, :, part], keys[other, :, part]], axis=0)
                value = jnp.concatenate(
                    [
                        jnp.concatenate([values[one, :, part], ones], axis=1),
                        jnp.concatenate([values[other, :, part], ones], axis=1) * there,
                    ],
                    axis=0,
                )
                q = query[:, part]
                stacked = jnp.concatenate([jnp.where(first, q, zero), jnp.where(first, zero, q)], axis=0)
                weights = jnp.exp2(contract_last(stacked, key)).astype(BF16)
                both = jnp.dot(weights, value, preferred_element_type=F32)
                acc_ref[0, :, part] += jnp.where(first, both[:tile_size, :lanes], both[tile_size:, :lanes])
                acc_ref[1, :, part] += jnp.where(first, both[:tile_size, lanes:], both[tile_size:, lanes:])
            return carry

        lax.fori_loop(0, (have + 1) // 2, step, 0)
        if last:
            t = tile_of[slot]
            a, b = t // tile_cols, t % tile_cols
            half = tile_size // 2
            nums = [acc_ref[0, s * half : (s + 1) * half] for s in range(2)]
            dens = [acc_ref[1, s * half : (s + 1) * half] for s in range(2)]
            finish(a, b, nums, dens, tokens_ref, wo_ref, staged.at[slot])
            copy_of(slot).start()
        else:
            acc_out_ref[slot] = acc_ref[...]
        return carry

    def copy_of(slot):
        t = tile_of[slot]
        a, b = t // tile_cols, t % tile_cols
        return pltpu.make_async_copy(
            staged.at[slot],
            out_ref.at[
                pl.ds(a * TILE_ROWS, TILE_ROWS), pl.ds(pl.multiple_of(b * TILE_COLS, TILE_COLS), TILE_COLS)
            ],
            sems.at[slot],
        )

    lax.fori_loop(0, slots, attend, 0)
    if last:
        def drain(slot, carry):
            copy_of(slot).wait()
            return carry

        lax.fori_loop(0, slots, drain, 0)


def body(
    tokens,
    norm_gain,
    query_weight,
    key_weight,
    value_weight,
    out_weight,
    head_scale,
    counts,
    sources,
):
    grid_rows, grid_cols, feature = tokens.shape
    tile_rows = grid_rows // TILE_ROWS
    tile_cols = grid_cols // TILE_COLS
    tiles = tile_rows * tile_cols
    tile_size = TILE_ROWS * TILE_COLS
    keep = tiles - min(4, MASK_MOST)
    col_count = lax.axis_size("col")
    vmem = pl.BlockSpec(memory_space=pltpu.VMEM)
    smem = pl.BlockSpec(memory_space=pltpu.SMEM)
    hbm = pl.BlockSpec(memory_space=pl.ANY)

    free = jnp.repeat(jnp.repeat(counts == 0, TILE_ROWS, axis=0), TILE_COLS, axis=1)[..., None]
    mark = jnp.asarray(MARK, tokens.dtype)
    left = jnp.where(free[:, :RADIUS], tokens[:, :RADIUS], mark)
    right = jnp.where(free[:, -RADIUS:], tokens[:, -RADIUS:], mark)
    before, after = pair_swap(left, right, "col")
    gap = jnp.full((grid_rows, TILE_COLS - 2 * RADIUS, feature), mark)
    tail = jnp.concatenate([after, gap, before], axis=1)
    upper = jnp.concatenate([jnp.where(free[:RADIUS], tokens[:RADIUS], mark), tail[:RADIUS]], axis=1)
    lower = jnp.concatenate([jnp.where(free[-RADIUS:], tokens[-RADIUS:], mark), tail[-RADIUS:]], axis=1)
    top, bottom = pair_swap(upper, lower, "row")

    sizes = (keep - LATE_TILES, LATE_TILES)
    packed = pl.pallas_call(
        functools.partial(pack_kernel, tile_cols, keep),
        out_shape=[jax.ShapeDtypeStruct((n, tile_size, feature), tokens.dtype) for n in sizes],
        in_specs=[smem, vmem],
        out_specs=[vmem] * 2,
        name="pack",
    )(counts, tokens)
    rel_counts = spread(counts, "col")
    early = spread(packed[0], "col")
    late = spread(packed[1], "col")

    gain = norm_gain.reshape(1, feature)
    scale = jnp.repeat(head_scale * LOG2E, feature // HEADS).reshape(1, feature)
    acc_shape = jax.ShapeDtypeStruct((MASK_MOST, 2, tile_size, feature), F32)
    mq_shape = jax.ShapeDtypeStruct((MASK_MOST, tile_size, feature), BF16)
    padded = grid_rows + 2 * RADIUS
    lanes = 2 * feature // HEADS
    out, acc, mq = pl.pallas_call(
        near_kernel,
        out_shape=[jax.ShapeDtypeStruct(tokens.shape, tokens.dtype), acc_shape, mq_shape],
        in_specs=[smem] + [vmem] * 10,
        out_specs=[vmem] * 3,
        scratch_shapes=[
            pltpu.VMEM((2, padded, grid_cols, feature), BF16),
            pltpu.VMEM((2, padded, grid_cols, feature), BF16),
            pltpu.VMEM((2, padded, grid_cols, lanes), BF16),
            pltpu.VMEM((tile_rows, grid_cols // SIDE, TILE_ROWS * SIDE, feature), BF16),
            pltpu.VMEM((feature, feature), BF16),
        ],
        cost_estimate=pl.CostEstimate(flops=20_000_000_000, bytes_accessed=20_000_000, transcendentals=3_000_000),
        name="near",
    )(counts, tokens, tail, top, bottom, gain, scale, query_weight, key_weight, value_weight, out_weight)

    me = jnp.stack([lax.axis_index("col"), lax.axis_index("row")]).astype(jnp.int32)
    rels = sorted(rel_counts)
    slots = MASK_MOST * S_MAX

    def far(chunks, acc, last):
        plan = {"rels": rels, "chunks": [name for name, _ in chunks]}
        args = [me, counts, sources] + [rel_counts[r] for r in rels] + [item for _, item in chunks]
        specs = [smem] * (3 + len(rels)) + [vmem] * len(chunks)
        args += [mq, acc, gain, key_weight, value_weight]
        specs += [vmem] * 5
        scratch = [
            pltpu.VMEM((slots + 1, tile_size, feature), BF16),
            pltpu.VMEM((slots + 1, tile_size, feature), BF16),
            pltpu.VMEM((feature, feature), BF16),
            pltpu.VMEM((2, tile_size, feature), BF16),
            pltpu.VMEM((2, tile_size, feature), F32),
            pltpu.SMEM((slots,), jnp.int32),
            pltpu.SMEM((col_count * tiles,), jnp.int32),
            pltpu.SMEM((MASK_MOST, S_MAX), jnp.int32),
            pltpu.SMEM((MASK_MOST,), jnp.int32),
            pltpu.SMEM((MASK_MOST,), jnp.int32),
        ]
        if last:
            args += [tokens, out_weight, out]
            specs += [vmem, vmem, hbm]
            scratch += [
                pltpu.VMEM((MASK_MOST, TILE_ROWS, TILE_COLS, feature), BF16),
                pltpu.SemaphoreType.DMA((MASK_MOST,)),
            ]
        return pl.pallas_call(
            functools.partial(far_kernel, plan, last, tile_cols * col_count, None),
            out_shape=jax.ShapeDtypeStruct(out.shape, out.dtype) if last else acc_shape,
            in_specs=specs,
            out_specs=hbm if last else vmem,
            scratch_shapes=scratch,
            input_output_aliases={len(args) - 1: 0} if last else {},
            cost_estimate=pl.CostEstimate(flops=5_000_000_000, bytes_accessed=10_000_000, transcendentals=1_000_000),
            name="far_last" if last else "far",
        )(*args)

    acc = far([((r, 0, sizes[0]), early[r]) for r in rels], acc, False)
    return far([((r, sizes[0], sizes[1]), late[r]) for r in rels], acc, True)


def solution(mesh):
    placed = (
        P(("slab", "row"), "col", None),
        P(),
        P(),
        P(),
        P(),
        P(),
        P(),
        P(("slab", "row"), "col"),
        P(("slab", "row"), "col", None),
    )
    return jax.shard_map(
        body, mesh=mesh, in_specs=placed, out_specs=P(("slab", "row"), "col", None), check_vma=False
    )
```

```python
import functools
import math
import jax
import jax.numpy as jnp
from jax import lax
from jax.experimental import pallas as pl
from jax.experimental.pallas import tpu as pltpu
from jax.sharding import PartitionSpec as P

HEADS = 6
TILE_ROWS = 8
TILE_COLS = 16
RADIUS = 3
S_MAX = 4
MASK_MOST = 8
SIDE = 8
MARK = 1024.0
MARK_LEVEL = 1000.0
LATE_TILES = 4
GAP = 2
LOG2E = math.log2(math.e)
F32 = jnp.float32
BF16 = jnp.bfloat16


def pair_swap(low, high, axis):
    count = lax.axis_size(axis)
    index = lax.axis_index(axis)
    even = index % 2 == 0
    first = [(i, i + 1) for i in range(0, count - 1, 2)]
    second = [(i, i + 1) for i in range(1, count - 1, 2)]
    both = lambda pairs: pairs + [(b, a) for a, b in pairs]
    one = lax.ppermute(jnp.where(even, high, low), axis, both(first))
    two = lax.ppermute(jnp.where(even, low, high), axis, both(second))
    mark = jnp.asarray(MARK, low.dtype)
    before = jnp.where(index == 0, mark, jnp.where(even, two, one))
    after = jnp.where(index == count - 1, mark, jnp.where(even, one, two))
    return before, after


def spread(array, axis):
    count = lax.axis_size(axis)
    held = {0: array}
    bit = count // 2
    while bit:
        pairs = [(i, i ^ bit) for i in range(count)]
        held.update({rel ^ bit: lax.ppermute(item, axis, pairs) for rel, item in held.items()})
        bit //= 2
    return held


def pack_kernel(tile_cols, counts_ref, tokens_ref, *chunk_refs):
    tile_rows = tokens_ref.shape[0] // TILE_ROWS
    free = jnp.int32(0)
    for t in range(tile_rows * tile_cols):
        free = free + (counts_ref[t // tile_cols, t % tile_cols] == 0).astype(jnp.int32)
    seen_free = jnp.int32(0)
    seen_masked = jnp.int32(0)
    for t in range(tile_rows * tile_cols):
        a, b = t // tile_cols, t % tile_cols
        is_free = (counts_ref[a, b] == 0).astype(jnp.int32)
        rank = jnp.where(is_free == 1, seen_free, free + seen_masked)
        seen_free = seen_free + is_free
        seen_masked = seen_masked + 1 - is_free
        low = 0
        for ref in chunk_refs:
            size = ref.shape[0]

            @pl.when((rank >= low) & (rank < low + size))
            def _(ref=ref, low=low, a=a, b=b, rank=rank):
                ref[rank - low] = tokens_ref[
                    TILE_ROWS * a : TILE_ROWS * (a + 1), TILE_COLS * b : TILE_COLS * (b + 1), :
                ].reshape(TILE_ROWS * TILE_COLS, tokens_ref.shape[-1])

            low += size


def split_by(value, size):
    if size & (size - 1) == 0:
        return value >> (size.bit_length() - 1), value & (size - 1)
    return value // size, value % size


def plan_kernel(rels, all_cols, early_size, counts_ref, sources_ref, *refs):
    rel_counts = refs[: len(rels)]
    needed, totals, todo, todo_count, tile_of, place, ranks = refs[len(rels) :]
    tile_rows, tile_cols = counts_ref.shape
    tiles = tile_rows * tile_cols
    my_col = lax.axis_index("col")
    my_band = lax.axis_index("row")
    for rel, ref in zip(rels, rel_counts):
        rank = jnp.int32(0)
        for t in range(tiles):
            ranks[rel * tiles + t] = rank
            place[rel * tiles + t] = -1
            rank = rank + (ref[t // tile_cols, t % tile_cols] == 0).astype(jnp.int32)
    for slot in range(MASK_MOST):
        todo_count[0, slot] = 0
        todo_count[1, slot] = 0
    totals[0] = 0
    totals[1] = 0

    def plan_tile(t, slot):
        a, b = split_by(t, tile_cols)
        live = counts_ref[a, b]
        tile_of[jnp.where(live > 0, slot, MASK_MOST)] = t

        def plan_entry(j, carry):
            row, col = split_by(sources_ref[a, b, j], all_cols)
            owner, sb = split_by(col, tile_cols)
            where = (owner ^ my_col) * tiles
            rank = ranks[where + (row - my_band * tile_rows) * tile_cols + sb]
            name = where + rank
            phase = (rank >= early_size).astype(jnp.int32)
            at = place[name]
            count = totals[phase]
            fresh = at < 0
            at = jnp.where(fresh, count, at)
            place[name] = at
            needed[phase, at] = name
            totals[phase] = count + fresh.astype(jnp.int32)
            n = todo_count[phase, slot]
            todo[phase, slot, n] = at
            todo_count[phase, slot] = n + 1
            return carry

        lax.fori_loop(0, live, plan_entry, 0)
        return slot + (live > 0).astype(jnp.int32)

    totals[2] = lax.fori_loop(0, tiles, plan_tile, jnp.int32(0))


def unit(projected):
    feature = projected.shape[-1]
    lanes = 2 * feature // HEADS
    low = lax.broadcasted_iota(jnp.int32, (projected.shape[0], lanes), 1) < lanes // 2
    parts = []
    for p in range(feature // lanes):
        part = projected[:, p * lanes : (p + 1) * lanes]
        square = part * part
        first = jnp.sum(jnp.where(low, square, 0.0), axis=-1, keepdims=True)
        second = jnp.sum(jnp.where(low, 0.0, square), axis=-1, keepdims=True)
        parts.append(part * lax.rsqrt(jnp.where(low, first, second) + 1e-6))
    return jnp.concatenate(parts, axis=-1)


def normed_of(raw, gain):
    level = jnp.mean(raw * raw, axis=-1, keepdims=True)
    return raw * lax.rsqrt(level + 1e-6) * gain, level


def contract_last(left, right):
    return lax.dot_general(left, right, (((1,), (1,)), ((), ())), preferred_element_type=F32)


def near_kernel(
    scale_ref, counts_ref, tokens_ref, tail_ref, top_ref, bottom_ref, gain_ref,
    wq_ref, wk_ref, wv_ref, wo_ref,
    out_ref, acc_ref, mq_ref,
    keys, values, valid, queries, attended, wkv,
):
    grid_rows, grid_cols, feature = tokens_ref.shape
    tile_rows = grid_rows // TILE_ROWS
    tile_cols = grid_cols // TILE_COLS
    wide = tail_ref.shape[1] + grid_cols
    lanes = 2 * feature // HEADS
    win_rows = TILE_ROWS + 2 * RADIUS
    gain = gain_ref[...].reshape(1, feature)
    wkv[:, :feature] = wk_ref[...]
    wkv[:, feature:] = wv_ref[...]
    head = lax.broadcasted_iota(jnp.int32, (1, feature), 1) // (feature // HEADS)
    scale = jnp.zeros((1, feature), F32)
    for h in range(HEADS):
        scale = jnp.where(head == h, scale_ref[h] * LOG2E, scale)

    def put_keys(raw, own_valid, places):
        rows = raw.shape[0]
        normed, level = normed_of(raw, gain[None])
        ok = jnp.where(level < MARK_LEVEL, own_valid, 0.0)
        ok = pltpu.roll(jnp.broadcast_to(ok, (rows, wide, lanes)), RADIUS, 1)
        shifted = pltpu.roll(normed, RADIUS, 1).reshape(rows * wide, feature).astype(BF16)
        both = jnp.dot(shifted, wkv[...], preferred_element_type=F32)
        key = unit(both[:, :feature]).reshape(rows, wide, feature)
        value = both[:, feature:].reshape(rows, wide, feature)
        value = value * jnp.concatenate([ok] * (feature // lanes), axis=-1)
        for side in range(2):
            low = side * SIDE
            for at, start, size in places:
                into = (side, pl.ds(at, size))
                keys[into] = key[start : start + size, low : low + grid_cols].astype(BF16)
                values[into] = value[start : start + size, low : low + grid_cols].astype(BF16)
                valid[into] = ok[start : start + size, low : low + grid_cols].astype(BF16)
        return normed

    edge = jnp.concatenate([top_ref[...], bottom_ref[...]], axis=0).astype(F32)
    put_keys(edge, 1.0, ((0, 0, RADIUS), (RADIUS + grid_rows, RADIUS, RADIUS)))

    def project(a, carry):
        rows = pl.ds(a * TILE_ROWS, TILE_ROWS)
        raw = jnp.concatenate([tokens_ref[rows].astype(F32), tail_ref[rows].astype(F32)], axis=1)
        tile = lax.broadcasted_iota(jnp.int32, (1, wide, 1), 1) // TILE_COLS
        own_valid = jnp.ones((1, wide, 1), F32)
        for b in range(tile_cols):
            flag = jnp.where(counts_ref[a, b] == 0, 1.0, 0.0)
            own_valid = jnp.where(tile == b, flag, own_valid)
        normed = put_keys(raw, own_valid, ((RADIUS + a * TILE_ROWS, 0, TILE_ROWS),))
        flat = normed[:, :grid_cols].astype(BF16).reshape(TILE_ROWS * grid_cols, feature)
        query = unit(jnp.dot(flat, wq_ref[...], preferred_element_type=F32)) * scale
        query = query.reshape(TILE_ROWS, grid_cols // SIDE, SIDE, feature)
        for c in range(grid_cols // SIDE):
            queries[a, c] = query[:, c].reshape(TILE_ROWS * SIDE, feature).astype(BF16)
        return carry

    lax.fori_loop(0, tile_rows, project, 0)

    tokens_of_side = TILE_ROWS * SIDE
    window = win_rows * TILE_COLS
    qpos = lax.broadcasted_iota(jnp.int32, (2 * tokens_of_side, window), 0) % tokens_of_side
    kpos = lax.broadcasted_iota(jnp.int32, (2 * tokens_of_side, window), 1)
    down = kpos // TILE_COLS - qpos // SIDE
    across = kpos % TILE_COLS - qpos % SIDE
    inside = (down >= 0) & (down <= 2 * RADIUS) & (across >= 0) & (across <= 2 * RADIUS)
    band = jnp.where(inside, 1.0, 0.0).astype(BF16)
    first = lax.broadcasted_iota(jnp.int32, (tokens_of_side, lanes), 1) < lanes // 2
    zero = jnp.zeros((tokens_of_side, lanes), BF16)

    def attend(a, slot):
        for b in range(tile_cols):
            masked = counts_ref[a, b] > 0
            into = jnp.where(masked, slot, MASK_MOST)
            slot = slot + masked.astype(jnp.int32)
            for p in range(feature // lanes):
                part = slice(p * lanes, (p + 1) * lanes)
                sides = []
                for side in range(2):
                    at = (side, pl.ds(a * TILE_ROWS, win_rows), slice(b * TILE_COLS, (b + 1) * TILE_COLS))
                    ok = valid[at].reshape(window, lanes)
                    key = keys[(*at, part)].reshape(window, lanes)
                    value = jnp.concatenate([values[(*at, part)].reshape(window, lanes), ok], axis=1)
                    q = queries[a, 2 * b + side, :, part]
                    stacked = jnp.concatenate([jnp.where(first, q, zero), jnp.where(first, zero, q)], axis=0)
                    weights = jnp.exp2(contract_last(stacked, key)).astype(BF16) * band
                    both = jnp.dot(weights, value, preferred_element_type=F32)
                    num = jnp.where(first, both[:tokens_of_side, :lanes], both[tokens_of_side:, :lanes])
                    den = jnp.where(first, both[:tokens_of_side, lanes:], both[tokens_of_side:, lanes:])
                    rows = slice(side * tokens_of_side, (side + 1) * tokens_of_side)
                    acc_ref[into, 0, rows, part] = num
                    acc_ref[into, 1, rows, part] = den
                    mq_ref[into, rows, part] = q
                    den = jnp.where(masked, 1.0, den)
                    sides.append((num / den).reshape(TILE_ROWS, SIDE, lanes))
                attended[
                    pl.ds(a * TILE_ROWS, TILE_ROWS), b * TILE_COLS : (b + 1) * TILE_COLS, part
                ] = jnp.concatenate(sides, axis=1).astype(BF16)
        return slot

    lax.fori_loop(0, tile_rows, attend, jnp.int32(0))

    def finish(a, carry):
        rows = pl.ds(a * TILE_ROWS, TILE_ROWS)
        flat = attended[rows].reshape(TILE_ROWS * grid_cols, feature)
        raw = tokens_ref[rows].reshape(TILE_ROWS * grid_cols, feature).astype(F32)
        mixed = raw + jnp.dot(flat, wo_ref[...], preferred_element_type=F32)
        out_ref[rows] = mixed.astype(BF16).reshape(TILE_ROWS, grid_cols, feature)
        return carry

    lax.fori_loop(0, tile_rows, finish, 0)


def far_kernel(rels, tiles, phase, low, group, *refs):
    needed, totals, todo, todo_count, tile_of = refs[:5]
    refs = refs[5:]
    chunks = dict(zip(rels, refs[: len(rels)]))
    refs = refs[len(rels) :]
    mq_hbm, gain_ref, wk_ref, wv_ref = refs[:4]
    refs = refs[4:]
    late = phase == 1
    if late:
        near_hbm, early_hbm, tokens_ref, wo_ref, _, out_hbm = refs[:6]
        refs = refs[6:]
    else:
        acc_hbm = refs[0]
        refs = refs[1:]
    keys, values, wkv, raw, mq, acc, fetch_sems, mq_sems, acc_sems = refs[:9]
    if late:
        near, staged, near_sems, out_sems = refs[9:]
    tile_size, feature = raw.shape[1:]
    lanes = 2 * feature // HEADS
    count = totals[phase]
    slots = totals[2]
    gain = gain_ref[...].reshape(1, feature)

    def fetch(i, carry):
        rel, rank = split_by(needed[phase, i], tiles)
        for known, ref in chunks.items():
            @pl.when(rel == known)
            def _(ref=ref):
                pltpu.make_async_copy(ref.at[rank - low], raw.at[i], fetch_sems.at[i]).start()

        return carry

    def mq_copy(slot):
        return pltpu.make_async_copy(mq_hbm.at[slot], mq.at[slot], mq_sems.at[slot])

    def near_copy(slot):
        return pltpu.make_async_copy(near_hbm.at[slot], near.at[slot], near_sems.at[slot])

    def acc_copy(slot):
        if late:
            return pltpu.make_async_copy(early_hbm.at[slot], acc.at[slot], acc_sems.at[slot])
        return pltpu.make_async_copy(acc.at[slot], acc_hbm.at[slot], acc_sems.at[slot])

    def each_slot(work, when=None):
        def run(slot, carry):
            if when is None:
                work(slot)
            else:
                pl.when(when(slot))(lambda: work(slot))
            return carry

        lax.fori_loop(0, slots, run, 0)

    had_early = lambda slot: todo_count[0, slot] > 0
    active = lambda slot: todo_count[phase, slot] > 0
    lax.fori_loop(0, count, fetch, 0)
    each_slot(lambda slot: mq_copy(slot).start(), active)
    if late:
        each_slot(lambda slot: acc_copy(slot).start(), had_early)
        each_slot(lambda slot: near_copy(slot).start())
    wkv[:, :feature] = wk_ref[...]
    wkv[:, feature:] = wv_ref[...]

    def project(i, carry):
        def arrived(k, carry):
            pltpu.make_async_copy(chunks[0].at[0], raw.at[k], fetch_sems.at[k]).wait()
            return carry

        lax.fori_loop(group * i, jnp.minimum(group * (i + 1), count), arrived, 0)
        at = pl.ds(group * i, group)
        flat = raw[at].reshape(group * tile_size, feature).astype(F32)
        normed = normed_of(flat, gain)[0].astype(BF16)
        both = jnp.dot(normed, wkv[...], preferred_element_type=F32)
        keys[at] = unit(both[:, :feature]).astype(BF16).reshape(group, tile_size, feature)
        values[at] = both[:, feature:].astype(BF16).reshape(group, tile_size, feature)
        return carry

    lax.fori_loop(0, (count + group - 1) // group, project, 0)
    each_slot(lambda slot: mq_copy(slot).wait(), active)
    if late:
        each_slot(lambda slot: acc_copy(slot).wait(), had_early)
        each_slot(lambda slot: near_copy(slot).wait())

        def join(slot, carry):
            @pl.when(had_early(slot))
            def _():
                near[slot] += acc[slot]

            return carry

        lax.fori_loop(0, slots, join, 0)

    first = lax.broadcasted_iota(jnp.int32, (tile_size, lanes), 1) < lanes // 2
    zero = jnp.zeros((tile_size, lanes), BF16)
    ones = jnp.ones((tile_size, lanes), BF16)

    def attend(slot, carry):
        have = todo_count[phase, slot]

        def wide(width):
            picks = [todo[phase, slot, jnp.minimum(k, have - 1)] for k in range(width)]
            there = [jnp.where(k < have, 1.0, 0.0).astype(BF16) for k in range(width)]
            for p in range(feature // lanes):
                part = slice(p * lanes, (p + 1) * lanes)
                key = jnp.concatenate([keys[at, :, part] for at in picks], axis=0)
                value = jnp.concatenate(
                    [jnp.concatenate([values[at, :, part], ones], axis=1) * is_there
                     for at, is_there in zip(picks, there)], axis=0)
                q = mq[slot, :, part]
                stacked = jnp.concatenate([jnp.where(first, q, zero), jnp.where(first, zero, q)], axis=0)
                weights = jnp.exp2(contract_last(stacked, key)).astype(BF16)
                both = jnp.dot(weights, value, preferred_element_type=F32)
                num = jnp.where(first, both[:tile_size, :lanes], both[tile_size:, :lanes])
                den = jnp.where(first, both[:tile_size, lanes:], both[tile_size:, lanes:])
                if late:
                    near[slot, 0, :, part] += num
                    near[slot, 1, :, part] += den
                else:
                    acc[slot, 0, :, part] = num
                    acc[slot, 1, :, part] = den

        pl.when((have > 0) & (have <= 2))(lambda: wide(2))
        pl.when(have > 2)(lambda: wide(S_MAX))
        if not late:
            pl.when(have > 0)(lambda: acc_copy(slot).start())
        return carry

    lax.fori_loop(0, slots, attend, 0)
    if not late:
        each_slot(lambda slot: acc_copy(slot).wait(), active)
        return

    tile_cols = tokens_ref.shape[1] // TILE_COLS

    def place_of(slot):
        a, b = split_by(tile_of[slot], tile_cols)
        return pl.ds(a * TILE_ROWS, TILE_ROWS), pl.ds(pl.multiple_of(b * TILE_COLS, TILE_COLS), TILE_COLS)

    def out_copy(slot):
        return pltpu.make_async_copy(staged.at[slot], out_hbm.at[place_of(slot)], out_sems.at[slot])

    def finish(slot, carry):
        half = tile_size // 2
        sides = []
        for side in range(2):
            rows = slice(side * half, (side + 1) * half)
            sides.append((near[slot, 0, rows] / near[slot, 1, rows]).reshape(TILE_ROWS, SIDE, feature))
        attended = jnp.concatenate(sides, axis=1).reshape(tile_size, feature).astype(BF16)
        mixed = tokens_ref[place_of(slot)].reshape(tile_size, feature).astype(F32) + jnp.dot(
            attended, wo_ref[...], preferred_element_type=F32
        )
        staged[slot] = mixed.astype(BF16).reshape(TILE_ROWS, TILE_COLS, feature)
        out_copy(slot).start()
        return carry

    lax.fori_loop(0, slots, finish, 0)
    each_slot(lambda slot: out_copy(slot).wait())


def body(
    tokens,
    norm_gain,
    query_weight,
    key_weight,
    value_weight,
    out_weight,
    head_scale,
    counts,
    sources,
):
    grid_rows, grid_cols, feature = tokens.shape
    tile_rows = grid_rows // TILE_ROWS
    tile_cols = grid_cols // TILE_COLS
    tiles = tile_rows * tile_cols
    tile_size = TILE_ROWS * TILE_COLS
    keep = tiles - min(4, MASK_MOST)
    col_count = lax.axis_size("col")
    vmem = pl.BlockSpec(memory_space=pltpu.VMEM)
    smem = pl.BlockSpec(memory_space=pltpu.SMEM)
    hbm = pl.BlockSpec(memory_space=pl.ANY)

    free = jnp.repeat(jnp.repeat(counts == 0, TILE_ROWS, axis=0), TILE_COLS, axis=1)[..., None]
    mark = jnp.asarray(MARK, tokens.dtype)
    left = jnp.where(free[:, :RADIUS], tokens[:, :RADIUS], mark)
    right = jnp.where(free[:, -RADIUS:], tokens[:, -RADIUS:], mark)
    with jax.named_scope("halo_col"):
        before, after = pair_swap(left, right, "col")
    gap = jnp.full((grid_rows, GAP, feature), mark)
    tail = jnp.concatenate([after, gap, before], axis=1)
    upper = jnp.concatenate([jnp.where(free[:RADIUS], tokens[:RADIUS], mark), tail[:RADIUS]], axis=1)
    lower = jnp.concatenate([jnp.where(free[-RADIUS:], tokens[-RADIUS:], mark), tail[-RADIUS:]], axis=1)
    with jax.named_scope("halo_row"):
        top, bottom = pair_swap(upper, lower, "row")

    sizes = (keep - LATE_TILES, LATE_TILES)
    packed = pl.pallas_call(
        functools.partial(pack_kernel, tile_cols),
        out_shape=[jax.ShapeDtypeStruct((n, tile_size, feature), tokens.dtype) for n in sizes],
        in_specs=[smem, vmem],
        out_specs=[vmem] * 2,
        name="pack",
    )(counts, tokens)
    with jax.named_scope("spread_counts"):
        rel_counts = spread(counts, "col")
    with jax.named_scope("spread_early"):
        early = spread(packed[0], "col")
    with jax.named_scope("spread_late"):
        late = spread(packed[1], "col")

    rels = sorted(rel_counts)
    slots = MASK_MOST * S_MAX
    ints = lambda *shape: jax.ShapeDtypeStruct(shape, jnp.int32)
    plan = pl.pallas_call(
        functools.partial(plan_kernel, rels, tile_cols * col_count, sizes[0]),
        out_shape=[ints(2, slots), ints(3), ints(2, MASK_MOST, S_MAX), ints(2, MASK_MOST), ints(MASK_MOST + 1)],
        in_specs=[smem] * (2 + len(rels)),
        out_specs=[smem] * 5,
        scratch_shapes=[pltpu.SMEM((col_count * tiles,), jnp.int32)] * 2,
        name="plan",
    )(counts, sources, *[rel_counts[r] for r in rels])

    acc_shape = jax.ShapeDtypeStruct((MASK_MOST, 2, tile_size, feature), F32)
    padded = grid_rows + 2 * RADIUS
    lanes = 2 * feature // HEADS
    out, acc, mq = pl.pallas_call(
        near_kernel,
        out_shape=[
            jax.ShapeDtypeStruct(tokens.shape, tokens.dtype),
            jax.ShapeDtypeStruct((MASK_MOST + 1, 2, tile_size, feature), F32),
            jax.ShapeDtypeStruct((MASK_MOST + 1, tile_size, feature), BF16),
        ],
        in_specs=[smem] * 2 + [vmem] * 9,
        out_specs=[vmem] * 3,
        scratch_shapes=[
            pltpu.VMEM((2, padded, grid_cols, feature), BF16),
            pltpu.VMEM((2, padded, grid_cols, feature), BF16),
            pltpu.VMEM((2, padded, grid_cols, lanes), BF16),
            pltpu.VMEM((tile_rows, grid_cols // SIDE, TILE_ROWS * SIDE, feature), BF16),
            pltpu.VMEM(tokens.shape, BF16),
            pltpu.VMEM((feature, 2 * feature), BF16),
        ],
        cost_estimate=pl.CostEstimate(flops=20_000_000_000, bytes_accessed=20_000_000, transcendentals=3_000_000),
        name="near",
    )(head_scale, counts, tokens, tail, top, bottom, norm_gain, query_weight, key_weight, value_weight, out_weight)

    def far(phase, chunks):
        group = 2 if phase else 4
        args = [*plan, *[chunks[r] for r in rels], mq, norm_gain, key_weight, value_weight]
        specs = [smem] * 5 + [hbm] * (len(rels) + 1) + [vmem] * 3
        sems = lambda n: pltpu.SemaphoreType.DMA((n,))
        scratch = [
            pltpu.VMEM((slots + group, tile_size, feature), BF16),
            pltpu.VMEM((slots + group, tile_size, feature), BF16),
            pltpu.VMEM((feature, 2 * feature), BF16),
            pltpu.VMEM((slots + group, tile_size, feature), BF16),
            pltpu.VMEM((MASK_MOST, tile_size, feature), BF16),
            pltpu.VMEM(acc_shape.shape, F32),
            sems(slots),
            sems(MASK_MOST),
            sems(MASK_MOST),
        ]
        if phase:
            args += [acc, early_acc, tokens, out_weight, out]
            specs += [hbm, hbm, vmem, vmem, hbm]
            scratch += [
                pltpu.VMEM(acc_shape.shape, F32),
                pltpu.VMEM((MASK_MOST, TILE_ROWS, TILE_COLS, feature), BF16),
                sems(MASK_MOST),
                sems(MASK_MOST),
            ]
        return pl.pallas_call(
            functools.partial(far_kernel, rels, tiles, phase, sizes[0] if phase else 0, group),
            out_shape=jax.ShapeDtypeStruct(out.shape, out.dtype) if phase else acc_shape,
            in_specs=specs,
            out_specs=hbm,
            scratch_shapes=scratch,
            input_output_aliases={len(args) - 1: 0} if phase else {},
            cost_estimate=pl.CostEstimate(flops=5_000_000_000, bytes_accessed=10_000_000, transcendentals=1_000_000),
            name="far_late" if phase else "far_early",
        )(*args)

    early_acc = far(0, early)
    return far(1, late)


def solution(mesh):
    placed = (
        P(("slab", "row"), "col", None),
        P(),
        P(),
        P(),
        P(),
        P(),
        P(),
        P(("slab", "row"), "col"),
        P(("slab", "row"), "col", None),
    )
    return jax.shard_map(
        body, mesh=mesh, in_specs=placed, out_specs=P(("slab", "row"), "col", None), check_vma=False
    )
```
